1024 devices in a mesh: head: 16 (over y, core), inner: 16 (over z_hi, x), outer: 4 (over z_lo).
Axes of the slice: x: 4, y: 8, z: 16 (z_hi: 4, z_lo: 4; z = z_hi * 4 + z_lo), core: 2. Of those that a mesh axis runs over, the one named last changes fastest.
Arguments:
- activations: bfloat16 [8192, 8192], P(('inner', 'outer')), may hold values from -6 to 6
- key_matrix: bfloat16 [8192, 512], P('inner'), may hold values from -0.0625 to 0.0625
- value_matrix: bfloat16 [8192, 512], P('inner'), may hold values from -0.0625 to 0.0625
- queries: bfloat16 [8192, 4096], P(('inner', 'outer'), 'head'), may hold values from -160 to 160
- block_order: int32 [128], replicated, may hold values from 0 to 127, each once
Outputs:
- attended: bfloat16 [64, 16, 8, 4096], P(('inner', 'outer'), 'head')
The draws below stay inside these ranges and needn't reach their ends.
Inputs may be any that keep to these rules, and one draw needn't show every extreme that they name: `block_order`: every block number appears once.
All inputs are finite; a program needn't handle non-finite values.
Results may differ from the reference program's by a relative error of at most 0.011.
Values may be sent and summed in bfloat16 or wider, within the bound.
A program may use at most 32 MiB of HBM per device.

```python
import math
import jax
import jax.numpy as jnp
from jax import lax

MODEL_WIDTH = 8192
QUERY_HEADS = 32
KEY_VALUE_HEADS = 4
HEAD_WIDTH = 128
TOK = 128
SEQ = 8192
CYCLE = 64
NBLK = 128
SUB = 8
N_HEAD = 16


def draw_queries(key, part):
    first_key = jax.random.fold_in(key, 0)
    return jnp.clip(2.5 * jax.random.normal(first_key, (SEQ, QUERY_HEADS * HEAD_WIDTH), jnp.float32), -15.0, 15.0).astype(jnp.bfloat16)


def block_levels(key, dims, cuts, least, high):
    level, own = 1.0, jax.random.fold_in(key, 6)
    for position, shards_of in cuts:
        draws = jnp.exp(jax.random.uniform(jax.random.fold_in(own, position), (shards_of,), jnp.float32, least / len(cuts), high / len(cuts)))
        level = level * jnp.repeat(draws, dims[position] // shards_of).reshape([-1 if axis == position else 1 for axis in range(len(dims))])
    return level


def scatter_about(rng, dims, scale, bound, cuts=(), held_as=jnp.bfloat16):
    loudness = block_levels(rng, dims, cuts, -0.22, 0.18) if cuts else 1.0
    drawn = jax.random.normal(rng, dims, jnp.float32) * scale * loudness
    return jnp.minimum(jnp.maximum(drawn, -bound), bound).astype(held_as)


def setup_inputs(seed: int = 0) -> dict:
    key_of = jax.random.split(jax.random.key(seed), 6)
    activations = scatter_about(key_of[0], (SEQ, MODEL_WIDTH), 1.0, 6.0, ((0, 64),))
    key_matrix = scatter_about(key_of[1], (MODEL_WIDTH, KEY_VALUE_HEADS * HEAD_WIDTH), MODEL_WIDTH ** -0.5, 0.0625, ((0, 16),))
    value_matrix = scatter_about(key_of[2], (MODEL_WIDTH, KEY_VALUE_HEADS * HEAD_WIDTH), MODEL_WIDTH ** -0.5, 0.0625, ((0, 16),))
    queries = draw_queries(jax.random.fold_in(key_of[5], 71), 0)
    block_order = jax.random.permutation(key_of[4], NBLK).astype(jnp.int32)
    return {"activations": activations, "key_matrix": key_matrix, "value_matrix": value_matrix, "queries": queries, "block_order": block_order}


def reference(activations, key_matrix, value_matrix, queries, block_order):
    keys = jnp.dot(activations, key_matrix, preferred_element_type=jnp.float32).astype(jnp.bfloat16)
    values = jnp.dot(activations, value_matrix, preferred_element_type=jnp.float32).astype(jnp.bfloat16)
    block_size = TOK // 2
    positions = (block_order[:, None] * block_size + jnp.arange(block_size, dtype=jnp.int32)[None, :]).reshape(SEQ)
    allowed = positions[None, :] <= positions[:, None]
    heads_per_group = QUERY_HEADS // KEY_VALUE_HEADS
    score_scale = 1.0 / math.sqrt(HEAD_WIDTH)

    def one_head(head):
        query_rows = lax.dynamic_slice_in_dim(queries, (head * HEAD_WIDTH).astype(jnp.int32), HEAD_WIDTH, 1)
        kv_head = (head // heads_per_group).astype(jnp.int32)
        key_rows = lax.dynamic_slice_in_dim(keys, kv_head * HEAD_WIDTH, HEAD_WIDTH, 1)
        value_rows = lax.dynamic_slice_in_dim(values, kv_head * HEAD_WIDTH, HEAD_WIDTH, 1)
        scores = jnp.dot(query_rows, key_rows.T, preferred_element_type=jnp.float32) * score_scale
        row_max = lax.optimization_barrier(jnp.max(jnp.where(allowed, scores, -1e+30), axis=1, keepdims=True))
        unnormed = jnp.where(allowed, jnp.exp(scores - row_max), 0.0)
        totals = lax.optimization_barrier(jnp.sum(unnormed, axis=1))
        mixed = jnp.dot(unnormed.astype(jnp.bfloat16), value_rows, preferred_element_type=jnp.float32)
        return mixed / totals[:, None]
    heads_out = lax.map(one_head, jnp.arange(QUERY_HEADS, dtype=jnp.int32))
    attended = jnp.transpose(heads_out, (1, 0, 2)).reshape(SEQ, QUERY_HEADS * HEAD_WIDTH).astype(jnp.bfloat16)
    return attended.reshape(CYCLE, N_HEAD, SUB, QUERY_HEADS * HEAD_WIDTH)
```

```python
import functools
import math

import jax
import jax.numpy as jnp
from jax import lax
from jax.experimental import pallas as pl
from jax.experimental.pallas import tpu as pltpu
from jax.sharding import PartitionSpec as P

D = 128
TOK = 128
BLK = 64
NX = 4
NZ = 16
LOW = -1e30
FLOOR = -1e28
MESH = pl.DeviceIdType.MESH
BF = jnp.bfloat16
F32 = jnp.float32
ARRIVE = (0, 15, 1, 14, 2, 13, 3, 12, 4, 11, 5, 10, 6, 9, 7, 8)


def kernel(
    nh, act, kmat, vmat, queries, order, out,
    act_v, wraw, w, acc, kv, qbuf, kpos, qpos, oout, oin, sout, sin, fin,
    lsem, wsend, wrecv, zsend, krecv, ysend, csend, qsend, qrecv, osend, orecv, ssend, srecv, asend, arecv,
):
    head = lax.axis_index("head")
    inner = lax.axis_index("inner")
    outer = lax.axis_index("outer")
    y, c = lax.div(head, 2), lax.rem(head, 2)
    k, x = lax.div(inner, NX), lax.rem(inner, NX)
    z = k * 4 + outer
    group = lax.div(y, 2)
    side = lax.rem(y, 2)

    def at_z(step):
        return lax.rem(z + step + NZ, NZ)

    def at_x(step):
        return lax.rem(x + step + NX, NX)

    def at_k(step):
        return lax.rem(k + step + 4, 4)

    def dev_xz(px, pz):
        return (head, lax.div(pz, 4) * NX + px, lax.rem(pz, 4))

    def dev_h(h):
        return (h, inner, outer)

    y_mate = dev_h((y + 1 - 2 * side) * 2 + c)
    c_mate = dev_h(y * 2 + 1 - c)

    def load(src, dst, n):
        cp = pltpu.make_async_copy(src, dst, lsem.at[n])
        cp.start()
        return cp

    cols = pl.ds(pl.multiple_of(group * D, D), D)

    @pl.when(side == 0)
    def _():
        load(kmat.at[:, cols], wraw, 0)

    @pl.when(side == 1)
    def _():
        load(vmat.at[:, cols], wraw, 0)

    act_cp = load(act, act_v, 1)
    q_cp = load(queries, qbuf.at[x], 2)

    sin[...] = jnp.zeros_like(sin)

    barrier = pltpu.get_barrier_semaphore()
    peers = [dev_xz(x, at_z(s)) for s in (-4, 4, -3, 3, -2, 2, -1, 1)]
    peers += [dev_xz(at_x(s), z) for s in (1, 2, 3)]
    for p in peers:
        pl.semaphore_signal(barrier, inc=1, device_id=p, device_id_type=MESH)

    def greet(s, carry):
        pl.semaphore_signal(barrier, inc=1, device_id=dev_h(lax.rem(head + s, nh)), device_id_type=MESH)
        return carry

    lax.fori_loop(1, nh, greet, 0)

    pltpu.make_async_copy(kmat.at[:, cols], wraw, lsem.at[0]).wait()
    lane = lax.broadcasted_iota(jnp.int32, (256, D), 1)
    left = lane < BLK
    top, bottom = wraw[0:256, :].astype(F32), wraw[256:512, :].astype(F32)
    direct = jnp.where(left, top, bottom)
    rolled = jnp.where(left, pltpu.roll(top, BLK, 1), pltpu.roll(bottom, BLK, 1))
    straight = (lane >= BLK).astype(jnp.int32) == jnp.full((256, D), c, jnp.int32)
    w[k, x] = jnp.where(straight, direct, rolled).astype(BF)

    pl.semaphore_wait(barrier, len(peers) + nh - 1)

    started = []

    def wcopy(bk, bx, half, n, device):
        part = w.at[bk, bx, pl.ds(half * 128, 128)]
        return pltpu.make_async_remote_copy(
            part, part, wsend.at[n], wrecv.at[bk, bx, half], device_id=device, device_id_type=MESH
        )

    def wput(bk, bx, half, device):
        cp = wcopy(bk, bx, half, len(started), device)
        started.append(cp)
        cp.start()

    def wgot(bk, bx, half):
        wcopy(bk, bx, half, 0, c_mate).wait_recv()

    right, left_z = dev_xz(x, at_z(4)), dev_xz(x, at_z(-4))
    x_up, x_down = dev_xz(at_x(1), z), dev_xz(at_x(-1), z)
    xu, xd, xo = at_x(1), at_x(-1), at_x(2)
    ku, kd, ko = at_k(1), at_k(-1), at_k(2)

    def spread(bk, half):
        wput(bk, x, half, x_up)
        wput(bk, x, half, x_down)

    def pass_on(bk):
        wgot(bk, xd, 0)
        wput(bk, xd, 0, x_up)
        wgot(bk, xu, 1)
        wput(bk, xu, 1, x_down)

    wput(k, x, 0, right)
    wput(k, x, 1, left_z)
    wput(k, x, 1, right)
    wput(k, x, 0, left_z)
    wput(k, x, 0, x_up)
    wput(k, x, 1, x_down)
    wput(k, x, 1, x_up)
    wput(k, x, 0, x_down)
    pass_on(k)

    lanes = lax.broadcasted_iota(jnp.int32, (1, D), 1)
    for zz in range(NZ):
        first = (((zz // 4) * NX + x) * 4 + zz % 4) * 2
        b0, b1 = order[first], order[first + 1]
        kpos[0:1, zz * TOK : (zz + 1) * TOK] = jnp.where(
            lanes < BLK, b0 * BLK + lanes, b1 * BLK + lanes - BLK
        )
    rows = lax.broadcasted_iota(jnp.int32, (TOK, D), 0)
    for xx in range(NX):
        first = ((k * NX + xx) * 4 + outer) * 2
        b0, b1 = order[first], order[first + 1]
        qpos[xx] = jnp.where(rows < BLK, b0 * BLK + rows, b1 * BLK + rows - BLK)

    act_cp.wait()
    acc[...] = jnp.zeros_like(acc)

    def project(bk, bx):
        base = (bk * NX + bx) * 512
        for i in range(2):
            rows_of = act_v[:, pl.ds(pl.multiple_of(base + i * 256, 256), 256)]
            acc[i] += jnp.dot(rows_of, w[bk, bx], preferred_element_type=F32)

    project(k, x)

    wgot(kd, x, 0)
    wput(kd, x, 0, right)
    spread(kd, 0)
    wgot(ku, x, 1)
    wput(ku, x, 1, left_z)
    spread(ku, 1)
    wgot(kd, x, 1)
    spread(kd, 1)
    wgot(ku, x, 0)
    spread(ku, 0)

    q_cp.wait()
    q_sent = []
    for i, s in enumerate((2, 1, 3)):
        cp = pltpu.make_async_remote_copy(
            qbuf.at[x], qbuf.at[x], qsend.at[i], qrecv.at[x],
            device_id=dev_xz(at_x(s), z), device_id_type=MESH,
        )
        cp.start()
        q_sent.append(cp)

    def finish(bk, around):
        if around:
            wgot(bk, xd, 1)
            project(bk, xd)
            wgot(bk, xu, 0)
            project(bk, xu)
            wgot(bk, xo, 0)
            wgot(bk, xo, 1)
            project(bk, xo)

    finish(k, True)
    project(kd, x)
    project(ku, x)
    pass_on(kd)
    pass_on(ku)
    wgot(ko, x, 0)
    spread(ko, 0)
    wgot(ko, x, 1)
    spread(ko, 1)
    project(ko, x)
    finish(kd, True)
    finish(ku, True)
    pass_on(ko)
    finish(ko, True)

    product = acc[0] + pltpu.roll(acc[1], BLK, 1)
    own = pl.ds(pl.multiple_of(c * BLK, BLK), BLK)
    kv[side, own, pl.ds(pl.multiple_of(z * TOK, TOK), TOK)] = product.T[0:BLK, :].astype(BF)

    def piece(sd, cc, zz, lo=0, n=BLK):
        return kv.at[sd, pl.ds(pl.multiple_of(cc * BLK + lo, 32), n), pl.ds(pl.multiple_of(zz * TOK, TOK), TOK)]

    def kcopy(sd, cc, zz, send, device, lo=0, n=BLK):
        part = piece(sd, cc, zz, lo, n)
        return pltpu.make_async_remote_copy(
            part, part, send, krecv.at[sd, cc, zz], device_id=device, device_id_type=MESH
        )

    zsent, ysent = [], []

    def zput(zz, device, lo=0, n=BLK):
        cp = kcopy(side, c, zz, zsend.at[len(zsent)], device, lo, n)
        zsent.append(cp)
        cp.start()

    def kgot(sd, cc, zz):
        kcopy(sd, cc, zz, zsend.at[0], c_mate).wait_recv()

    def yput(zz):
        i = len(ysent)
        for cp in (
            kcopy(side, c, zz, ysend.at[i], y_mate),
            kcopy(side, c, zz, csend.at[0, i], c_mate),
        ):
            cp.start()
        ysent.append((side, c, zz, i))

    for s in (4, -4, 3, -3, 2, -2, 1, -1):
        zput(z, dev_xz(x, at_z(s)))

    passed = []

    def relay(zz):
        i = len(passed)
        kgot(1 - side, c, zz)
        kcopy(1 - side, c, zz, csend.at[1, i], c_mate).start()
        passed.append(zz)

    order_z = [at_z(s) for s in ARRIVE]
    lag = 3
    for i in range(NZ):
        zz = order_z[i]
        if i:
            kgot(side, c, zz)
        if ARRIVE[i] == 12:
            zput(zz, dev_xz(x, at_z(4)), 0, 32)
            for s in (3, 2, 1):
                zput(zz, dev_xz(x, at_z(s)))
        if ARRIVE[i] == 4:
            zput(zz, dev_xz(x, at_z(-4)), 32, 32)
            for s in (-3, -2, -1):
                zput(zz, dev_xz(x, at_z(s)))
        yput(zz)
        if i >= lag:
            relay(order_z[i - lag])
    for i in range(NZ - lag, NZ):
        relay(order_z[i])
    for zz in order_z:
        kgot(side, 1 - c, zz)
        kgot(1 - side, 1 - c, zz)

    scale = 1.0 / math.sqrt(D)
    stat_lane = lax.broadcasted_iota(jnp.int32, (TOK, D), 1)

    def attend(xq):
        stats = jnp.zeros((TOK, D), F32)
        allowed = kpos[0:1, :] <= qpos[xq][:, 0:1]
        for hh in range(2):
            q = qbuf[xq, :, hh * D : (hh + 1) * D]
            s = jnp.dot(q, kv[0], preferred_element_type=F32)
            s = jnp.where(allowed, s, LOW)
            m = jnp.maximum(jnp.max(s, axis=1, keepdims=True), FLOOR)
            p = jnp.exp((s - m) * scale)
            total = jnp.sum(p, axis=1, keepdims=True)
            o = lax.dot_general(
                p.astype(BF), kv[1], (((1,), (1,)), ((), ())), preferred_element_type=F32
            )
            o = o / jnp.maximum(total, 1e-30)
            oout[xq, :, hh * D : (hh + 1) * D] = o.astype(BF)
            stats = jnp.where(stat_lane == 2 * hh, m, stats)
            stats = jnp.where(stat_lane == 2 * hh + 1, total, stats)
        sout[xq] = stats.T[0:8, :]

    def ocopy(xq, xs, i, device):
        return (
            pltpu.make_async_remote_copy(
                oout.at[xq], oin.at[xs], osend.at[i], orecv.at[xs], device_id=device, device_id_type=MESH
            ),
            pltpu.make_async_remote_copy(
                sout.at[xq], sin.at[pl.ds(pl.multiple_of(xs * 8, 8), 8)], ssend.at[i], srecv.at[xs],
                device_id=device, device_id_type=MESH,
            ),
        )

    for s in (2, 1, 3):
        pltpu.make_async_remote_copy(
            qbuf.at[x], qbuf.at[at_x(s)], qsend.at[0], qrecv.at[at_x(s)], device_id=c_mate, device_id_type=MESH
        ).wait_recv()
    def step(i, carry):
        xq = lax.rem(x + 6 - i, NX)
        attend(xq)

        @pl.when(i != 2)
        def _():
            for cp in ocopy(xq, x, i, dev_xz(xq, z)):
                cp.start()

        return carry

    lax.fori_loop(0, NX, step, 0)
    for s in (2, 1, 3):
        for cp in ocopy(at_x(s), at_x(s), 0, c_mate):
            cp.wait_recv()
    oin[x] = oout[x]
    sin[pl.ds(pl.multiple_of(x * 8, 8), 8), :] = sout[x]

    st = sin[...].T
    for hh in range(2):
        ms = [st[:, 8 * i + 2 * hh : 8 * i + 2 * hh + 1] for i in range(NX)]
        ls = [st[:, 8 * i + 2 * hh + 1 : 8 * i + 2 * hh + 2] for i in range(NX)]
        top_m = functools.reduce(jnp.maximum, ms)
        ws = [l * jnp.exp((m - top_m) * scale) for m, l in zip(ms, ls)]
        denom = functools.reduce(jnp.add, ws)
        mixed = functools.reduce(
            jnp.add,
            [(wt / denom) * oin[i, :, hh * D : (hh + 1) * D].astype(F32) for i, wt in enumerate(ws)],
        )
        fin[:, :, hh * D : (hh + 1) * D] = mixed.reshape(TOK // 8, 8, D).astype(BF)

    def acopy(j, h, i, device):
        return pltpu.make_async_remote_copy(
            fin.at[j], out.at[:, pl.ds(pl.multiple_of(h * 2 * D, 2 * D), 2 * D)],
            asend.at[i], arecv.at[h], device_id=device, device_id_type=MESH,
        )

    def scatter(s, carry):
        j = lax.rem(head + s, nh)
        acopy(j, head, s, dev_h(j)).start()
        return carry

    lax.fori_loop(1, nh, scatter, 0)
    out[:, pl.ds(pl.multiple_of(head * 2 * D, 2 * D), 2 * D)] = fin[head]

    for cp in started + q_sent + zsent:
        cp.wait_send()
    for sd, cc, zz, i in ysent:
        kcopy(sd, cc, zz, ysend.at[i], y_mate).wait_send()
        kcopy(sd, cc, zz, csend.at[0, i], c_mate).wait_send()
    for i, zz in enumerate(passed):
        kcopy(1 - side, c, zz, csend.at[1, i], c_mate).wait_send()
    for i in (0, 1, 3):
        xq = lax.rem(x + 6 - i, NX)
        for cp in ocopy(xq, x, i, dev_xz(xq, z)):
            cp.wait_send()

    def close(s, carry):
        j = lax.rem(head + s, nh)
        cp = acopy(j, j, s, dev_h(j))
        cp.wait_send()
        cp.wait_recv()
        return carry

    lax.fori_loop(1, nh, close, 0)


def layer(nh, activations, key_matrix, value_matrix, queries, block_order):
    dma = pltpu.SemaphoreType.DMA
    anywhere = pl.BlockSpec(memory_space=pl.ANY)
    result = pl.pallas_call(
        functools.partial(kernel, nh),
        out_shape=jax.ShapeDtypeStruct((8, nh * 2 * D), BF),
        in_specs=[anywhere] * 4 + [pl.BlockSpec(memory_space=pltpu.SMEM)],
        out_specs=pl.BlockSpec(memory_space=pltpu.VMEM),
        scratch_shapes=[
            pltpu.VMEM((TOK, 8192), BF),
            pltpu.VMEM((512, D), BF),
            pltpu.VMEM((4, NX, 256, D), BF),
            pltpu.VMEM((2, TOK, D), F32),
            pltpu.VMEM((2, D, NZ * TOK), BF),
            pltpu.VMEM((NX, TOK, 2 * D), BF),
            pltpu.VMEM((8, NZ * TOK), jnp.int32),
            pltpu.VMEM((NX, TOK, D), jnp.int32),
            pltpu.VMEM((NX, TOK, 2 * D), BF),
            pltpu.VMEM((NX, TOK, 2 * D), BF),
            pltpu.VMEM((NX, 8, D), F32),
            pltpu.VMEM((D, D), F32),
            pltpu.VMEM((TOK // 8, 8, 2 * D), BF),
            dma((3,)),
            dma((30,)),
            dma((4, NX, 2)),
            dma((16,)),
            dma((2, 2, NZ)),
            dma((NZ,)),
            dma((2, NZ)),
            dma((3,)),
            dma((NX,)),
            dma((NX,)),
            dma((NX,)),
            dma((NX,)),
            dma((NX,)),
            dma((nh,)),
            dma((nh,)),
        ],
        compiler_params=pltpu.CompilerParams(collective_id=0, has_side_effects=True),
    )(activations, key_matrix, value_matrix, queries, block_order)
    return result.reshape(1, 1, 8, nh * 2 * D)


def solution(mesh):
    placed = (
        P(("inner", "outer"), None),
        P("inner", None),
        P("inner", None),
        P(("inner", "outer"), "head"),
        P(),
    )
    return jax.shard_map(
        functools.partial(layer, mesh.shape["head"]),
        mesh=mesh,
        in_specs=placed,
        out_specs=P(("inner", "outer"), "head", None, None),
        check_vma=False,
    )
```

```python
import functools
import math

import jax
import jax.numpy as jnp
from jax import lax
from jax.experimental import pallas as pl
from jax.experimental.pallas import tpu as pltpu
from jax.sharding import PartitionSpec as P

D = 128
TOK = 128
BLK = 64
NX = 4
NZ = 16
LOW = -1e30
FLOOR = -1e28
MESH = pl.DeviceIdType.MESH
BF = jnp.bfloat16
F32 = jnp.float32
ARRIVE = (0, 15, 1, 14, 2, 13, 3, 12, 4, 11, 5, 10, 6, 9, 7, 8)
SLOT = {offset: slot for slot, offset in enumerate(ARRIVE)}
NEAR = 9


def kernel(
    nh, act, kmat, vmat, queries, order, out,
    act_v, wraw, w, acc, kv, qbuf, kpos, qpos, mold, lold, aold, oout, oin, sout, sin, fin,
    lsem, wsend, wrecv, zsend, krecv, ysend, csend, qsend, qrecv, osend, orecv, ssend, srecv, asend, arecv,
):
    head = lax.axis_index("head")
    inner = lax.axis_index("inner")
    outer = lax.axis_index("outer")
    y, c = lax.div(head, 2), lax.rem(head, 2)
    k, x = lax.div(inner, NX), lax.rem(inner, NX)
    z = k * 4 + outer
    group = lax.div(y, 2)
    side = lax.rem(y, 2)

    def at_z(step):
        return lax.rem(z + step + NZ, NZ)

    def at_x(step):
        return lax.rem(x + step + NX, NX)

    def at_k(step):
        return lax.rem(k + step + 4, 4)

    def dev_xz(px, pz):
        return (head, lax.div(pz, 4) * NX + px, lax.rem(pz, 4))

    def dev_h(h):
        return (h, inner, outer)

    y_mate = dev_h((y + 1 - 2 * side) * 2 + c)
    c_mate = dev_h(y * 2 + 1 - c)

    def load(src, dst, n):
        cp = pltpu.make_async_copy(src, dst, lsem.at[n])
        cp.start()
        return cp

    cols = pl.ds(pl.multiple_of(group * D, D), D)

    @pl.when(side == 0)
    def _():
        load(kmat.at[:, cols], wraw, 0)

    @pl.when(side == 1)
    def _():
        load(vmat.at[:, cols], wraw, 0)

    act_cp = load(act, act_v, 1)
    q_cp = load(queries, qbuf.at[x], 2)

    sin[...] = jnp.zeros_like(sin)

    barrier = pltpu.get_barrier_semaphore()
    peers = [dev_xz(x, at_z(s)) for s in (-4, 4, -3, 3, -2, 2, -1, 1)]
    peers += [dev_xz(at_x(s), z) for s in (1, 2, 3)]
    for p in peers:
        pl.semaphore_signal(barrier, inc=1, device_id=p, device_id_type=MESH)

    def greet(s, carry):
        pl.semaphore_signal(barrier, inc=1, device_id=dev_h(lax.rem(head + s, nh)), device_id_type=MESH)
        return carry

    lax.fori_loop(1, nh, greet, 0)

    pltpu.make_async_copy(kmat.at[:, cols], wraw, lsem.at[0]).wait()
    lane = lax.broadcasted_iota(jnp.int32, (256, D), 1)
    left = lane < BLK
    top, bottom = wraw[0:256, :].astype(F32), wraw[256:512, :].astype(F32)
    direct = jnp.where(left, top, bottom)
    rolled = jnp.where(left, pltpu.roll(top, BLK, 1), pltpu.roll(bottom, BLK, 1))
    straight = (lane >= BLK).astype(jnp.int32) == jnp.full((256, D), c, jnp.int32)
    w[k, x] = jnp.where(straight, direct, rolled).astype(BF)

    pl.semaphore_wait(barrier, len(peers) + nh - 1)

    started = []

    def wcopy(bk, bx, half, n, device):
        part = w.at[bk, bx, pl.ds(half * 128, 128)]
        return pltpu.make_async_remote_copy(
            part, part, wsend.at[n], wrecv.at[bk, bx, half], device_id=device, device_id_type=MESH
        )

    def wput(bk, bx, half, device):
        cp = wcopy(bk, bx, half, len(started), device)
        started.append(cp)
        cp.start()

    def wgot(bk, bx, half):
        wcopy(bk, bx, half, 0, c_mate).wait_recv()

    right, left_z = dev_xz(x, at_z(4)), dev_xz(x, at_z(-4))
    ku, kd, ko = at_k(1), at_k(-1), at_k(2)
    others = [dev_xz(at_x(s), z) for s in (2, 1, 3)]

    def spread(bk, half):
        for device in others:
            wput(bk, x, half, device)

    wput(k, x, 0, right)
    wput(k, x, 1, left_z)
    wput(k, x, 1, right)
    wput(k, x, 0, left_z)
    spread(k, 0)
    spread(k, 1)

    lanes = lax.broadcasted_iota(jnp.int32, (1, D), 1)
    for slot, offset in enumerate(ARRIVE):
        zz = at_z(offset)
        first = ((lax.div(zz, 4) * NX + x) * 4 + lax.rem(zz, 4)) * 2
        b0, b1 = order[first], order[first + 1]
        kpos[0:1, slot * TOK : (slot + 1) * TOK] = jnp.where(
            lanes < BLK, b0 * BLK + lanes, b1 * BLK + lanes - BLK
        )
    rows = lax.broadcasted_iota(jnp.int32, (TOK, D), 0)
    for xx in range(NX):
        first = ((k * NX + xx) * 4 + outer) * 2
        b0, b1 = order[first], order[first + 1]
        qpos[xx] = jnp.where(rows < BLK, b0 * BLK + rows, b1 * BLK + rows - BLK)

    act_cp.wait()
    acc[...] = jnp.zeros_like(acc)

    def project(bk, bx):
        base = (bk * NX + bx) * 512
        for i in range(2):
            rows_of = act_v[:, pl.ds(pl.multiple_of(base + i * 256, 256), 256)]
            acc[i] += jnp.dot(rows_of, w[bk, bx], preferred_element_type=F32)

    project(k, x)

    wgot(kd, x, 0)
    wput(kd, x, 0, right)
    spread(kd, 0)
    wgot(ku, x, 1)
    wput(ku, x, 1, left_z)
    spread(ku, 1)
    wgot(kd, x, 1)
    spread(kd, 1)
    wgot(ku, x, 0)
    spread(ku, 0)

    q_cp.wait()
    q_sent = []
    for i, s in enumerate((2, 1, 3)):
        cp = pltpu.make_async_remote_copy(
            qbuf.at[x], qbuf.at[x], qsend.at[i], qrecv.at[x],
            device_id=dev_xz(at_x(s), z), device_id_type=MESH,
        )
        cp.start()
        q_sent.append(cp)

    def rest(bk):
        for step in (1, 3, 2):
            bx = at_x(step)
            wgot(bk, bx, 0)
            wgot(bk, bx, 1)
            project(bk, bx)

    rest(k)
    for half in range(2):
        wgot(ko, x, half)
        spread(ko, half)
    for bk in (kd, ku, ko):
        project(bk, x)
    for bk in (kd, ku, ko):
        rest(bk)

    product = acc[0] + pltpu.roll(acc[1], BLK, 1)
    own = pl.ds(pl.multiple_of(c * BLK, BLK), BLK)
    kv[side, own, 0:TOK] = product.T[0:BLK, :].astype(BF)

    def piece(sd, cc, slot, lo=0, n=BLK):
        columns = slot * TOK if isinstance(slot, int) else pl.multiple_of(slot * TOK, TOK)
        return kv.at[sd, pl.ds(pl.multiple_of(cc * BLK + lo, 32), n), pl.ds(columns, TOK)]

    def kcopy(sd, cc, slot, send, device, to=None, lo=0, n=BLK):
        to = slot if to is None else to
        return pltpu.make_async_remote_copy(
            piece(sd, cc, slot, lo, n), piece(sd, cc, to, lo, n), send, krecv.at[sd, cc, to],
            device_id=device, device_id_type=MESH,
        )

    zsent = []

    def zput(offset, step, lo=0, n=BLK):
        to = SLOT[(offset - step) % NZ]
        cp = kcopy(side, c, SLOT[offset % NZ], zsend.at[len(zsent)], dev_xz(x, at_z(step)), to, lo, n)
        zsent.append(cp)
        cp.start()

    def kgot(sd, cc, slot):
        kcopy(sd, cc, slot, zsend.at[0], c_mate).wait_recv()

    def to_mates(slot):
        kcopy(side, c, slot, ysend.at[slot], y_mate).start()
        kcopy(side, c, slot, csend.at[0, slot], c_mate).start()

    def relay(slot):
        kgot(1 - side, c, slot)
        kcopy(1 - side, c, slot, csend.at[1, slot], c_mate).start()

    def take(slot):
        kgot(side, c, slot)
        to_mates(slot)

    zput(0, 4)
    zput(0, -4)
    to_mates(0)
    for s in (3, -3, 2, -2, 1, -1):
        zput(0, s)
    kgot(side, c, SLOT[12])
    zput(-4, 4, 0, 32)
    for s in (3, 2, 1):
        zput(-4, s)
    kgot(side, c, SLOT[4])
    zput(4, -4, 32, 32)
    for s in (-3, -2, -1):
        zput(4, s)
    to_mates(SLOT[12])
    to_mates(SLOT[4])
    for slot in range(1, 7):
        take(slot)
    for turn in range(3):
        take(NEAR + 2 * turn)
        take(NEAR + 2 * turn + 1)
        for slot in range(3 * turn, 3 * turn + 3):
            relay(slot)
    take(NZ - 1)
    for s in (2, 1, 3):
        pltpu.make_async_remote_copy(
            qbuf.at[x], qbuf.at[at_x(s)], qsend.at[0], qrecv.at[at_x(s)], device_id=c_mate, device_id_type=MESH
        ).wait_recv()
    for slot in range(NEAR):
        kgot(side, 1 - c, slot)
        kgot(1 - side, 1 - c, slot)

    factor = math.log2(math.e) / math.sqrt(D)
    stat_lane = lax.broadcasted_iota(jnp.int32, (TOK, D), 1)
    near, far = pl.ds(0, NEAR * TOK), pl.ds(NEAR * TOK, (NZ - NEAR) * TOK)

    def scores(xq, part):
        s = jnp.dot(both_heads(xq), kv[0, :, part], preferred_element_type=F32)
        allowed = kpos[0:1, part] <= qpos[xq][:, 0:1]
        return jnp.where(allowed[None], s.reshape(2, TOK, -1), LOW).reshape(s.shape)

    def mix(p, part):
        return lax.dot_general(
            p.astype(BF), kv[1, :, part], (((1,), (1,)), ((), ())), preferred_element_type=F32
        )

    def both_heads(xq):
        return jnp.concatenate([qbuf[xq, :, 0:D], qbuf[xq, :, D : 2 * D]], axis=0)

    def first_part(i, carry):
        xq = lax.rem(x + 3 - i, NX)
        s = scores(xq, near)
        m = jnp.maximum(jnp.max(s, axis=1, keepdims=True), FLOOR)
        p = jnp.exp2((s - m) * factor)
        mold[i] = jnp.broadcast_to(m, (2 * TOK, D))
        lold[i] = jnp.broadcast_to(jnp.sum(p, axis=1, keepdims=True), (2 * TOK, D))
        aold[i] = mix(p, near)
        for slot in (NEAR + 2 * i, NEAR + 2 * i + 1):

            @pl.when(slot < NZ)
            def _():
                relay(slot)

        return carry

    lax.fori_loop(0, NX, first_part, 0)
    for slot in range(NEAR, NZ):
        kgot(side, 1 - c, slot)
        kgot(1 - side, 1 - c, slot)

    def ocopy(xq, xs, i, device):
        return (
            pltpu.make_async_remote_copy(
                oout.at[xq], oin.at[xs], osend.at[i], orecv.at[xs], device_id=device, device_id_type=MESH
            ),
            pltpu.make_async_remote_copy(
                sout.at[xq], sin.at[pl.ds(pl.multiple_of(xs * 8, 8), 8)], ssend.at[i], srecv.at[xs],
                device_id=device, device_id_type=MESH,
            ),
        )

    def second_part(i, carry):
        xq = lax.rem(x + 3 - i, NX)
        s = scores(xq, far)
        before = mold[i][:, 0:1]
        m = jnp.maximum(jnp.max(s, axis=1, keepdims=True), before)
        p = jnp.exp2((s - m) * factor)
        fade = jnp.exp2((before - m) * factor)
        total = lold[i][:, 0:1] * fade + jnp.sum(p, axis=1, keepdims=True)
        o = ((aold[i] * fade + mix(p, far)) / jnp.maximum(total, 1e-30)).astype(BF)
        stats = jnp.zeros((TOK, D), F32)
        for hh in range(2):
            rows_of = slice(hh * TOK, (hh + 1) * TOK)
            oout[xq, :, hh * D : (hh + 1) * D] = o[rows_of]
            stats = jnp.where(stat_lane == 2 * hh, m[rows_of], stats)
            stats = jnp.where(stat_lane == 2 * hh + 1, total[rows_of], stats)
        sout[xq] = stats.T[0:8, :]

        @pl.when(i < NX - 1)
        def _():
            for cp in ocopy(xq, x, i, dev_xz(xq, z)):
                cp.start()

        return carry

    lax.fori_loop(0, NX, second_part, 0)
    for s in (1, 3, 2):
        for cp in ocopy(at_x(s), at_x(s), 0, c_mate):
            cp.wait_recv()
    oin[x] = oout[x]
    sin[pl.ds(pl.multiple_of(x * 8, 8), 8), :] = sout[x]

    st = sin[...].T
    for hh in range(2):
        ms = [st[:, 8 * i + 2 * hh : 8 * i + 2 * hh + 1] for i in range(NX)]
        ls = [st[:, 8 * i + 2 * hh + 1 : 8 * i + 2 * hh + 2] for i in range(NX)]
        top_m = functools.reduce(jnp.maximum, ms)
        ws = [l * jnp.exp2((m - top_m) * factor) for m, l in zip(ms, ls)]
        denom = functools.reduce(jnp.add, ws)
        mixed = functools.reduce(
            jnp.add,
            [(wt / denom) * oin[i, :, hh * D : (hh + 1) * D].astype(F32) for i, wt in enumerate(ws)],
        )
        fin[:, :, hh * D : (hh + 1) * D] = mixed.reshape(TOK // 8, 8, D).astype(BF)

    def acopy(j, h, i, device):
        return pltpu.make_async_remote_copy(
            fin.at[j], out.at[:, pl.ds(pl.multiple_of(h * 2 * D, 2 * D), 2 * D)],
            asend.at[i], arecv.at[h], device_id=device, device_id_type=MESH,
        )

    def scatter(s, carry):
        j = lax.rem(head + s, nh)
        acopy(j, head, s, dev_h(j)).start()
        return carry

    lax.fori_loop(1, nh, scatter, 0)
    own_rows = load(fin.at[head], out.at[:, pl.ds(pl.multiple_of(head * 2 * D, 2 * D), 2 * D)], 0)
    own_rows.wait()

    for cp in started + q_sent + zsent:
        cp.wait_send()
    for slot in range(NZ):
        kcopy(side, c, slot, ysend.at[slot], y_mate).wait_send()
        kcopy(side, c, slot, csend.at[0, slot], c_mate).wait_send()
        kcopy(1 - side, c, slot, csend.at[1, slot], c_mate).wait_send()
    for i in range(NX - 1):
        xq = lax.rem(x + 3 - i, NX)
        for cp in ocopy(xq, x, i, dev_xz(xq, z)):
            cp.wait_send()

    def close(s, carry):
        j = lax.rem(head + s, nh)
        cp = acopy(j, j, s, dev_h(j))
        cp.wait_send()
        cp.wait_recv()
        return carry

    lax.fori_loop(1, nh, close, 0)


def layer(nh, activations, key_matrix, value_matrix, queries, block_order):
    dma = pltpu.SemaphoreType.DMA
    stays = pl.BlockSpec(memory_space=pltpu.HBM)
    result = pl.pallas_call(
        functools.partial(kernel, nh),
        out_shape=jax.ShapeDtypeStruct((8, nh * 2 * D), BF),
        in_specs=[stays] * 4 + [pl.BlockSpec(memory_space=pltpu.SMEM)],
        out_specs=stays,
        scratch_shapes=[
            pltpu.VMEM((TOK, 8192), BF),
            pltpu.VMEM((512, D), BF),
            pltpu.VMEM((4, NX, 256, D), BF),
            pltpu.VMEM((2, TOK, D), F32),
            pltpu.VMEM((2, D, NZ * TOK), BF),
            pltpu.VMEM((NX, TOK, 2 * D), BF),
            pltpu.VMEM((8, NZ * TOK), jnp.int32),
            pltpu.VMEM((NX, TOK, D), jnp.int32),
            pltpu.VMEM((NX, 2 * TOK, D), F32),
            pltpu.VMEM((NX, 2 * TOK, D), F32),
            pltpu.VMEM((NX, 2 * TOK, D), F32),
            pltpu.VMEM((NX, TOK, 2 * D), BF),
            pltpu.VMEM((NX, TOK, 2 * D), BF),
            pltpu.VMEM((NX, 8, D), F32),
            pltpu.VMEM((D, D), F32),
            pltpu.VMEM((TOK // 8, 8, 2 * D), BF),
            dma((3,)),
            dma((30,)),
            dma((4, NX, 2)),
            dma((16,)),
            dma((2, 2, NZ)),
            dma((NZ,)),
            dma((2, NZ)),
            dma((3,)),
            dma((NX,)),
            dma((NX,)),
            dma((NX,)),
            dma((NX,)),
            dma((NX,)),
            dma((nh,)),
            dma((nh,)),
        ],
        compiler_params=pltpu.CompilerParams(collective_id=0, has_side_effects=True),
    )(activations, key_matrix, value_matrix, queries, block_order)
    return result.reshape(1, 1, 8, nh * 2 * D)


def solution(mesh):
    placed = (
        P(("inner", "outer"), None),
        P("inner", None),
        P("inner", None),
        P(("inner", "outer"), "head"),
        P(),
    )
    return jax.shard_map(
        functools.partial(layer, mesh.shape["head"]),
        mesh=mesh,
        in_specs=placed,
        out_specs=P(("inner", "outer"), "head", None, None),
        check_vma=False,
    )
```

```python
import functools
import math

import jax
import jax.numpy as jnp
from jax import lax
from jax.experimental import pallas as pl
from jax.experimental.pallas import tpu as pltpu
from jax.sharding import PartitionSpec as P

D = 128
TOK = 128
BLK = 64
NX = 4
NZ = 16
LOW = -1e30
FLOOR = -1e28
MESH = pl.DeviceIdType.MESH
BF = jnp.bfloat16
F32 = jnp.float32
ARRIVE = (0, 15, 1, 14, 2, 13, 3, 12, 4, 11, 5, 10, 6, 9, 7, 8)
SLOT = {offset: slot for slot, offset in enumerate(ARRIVE)}
NEAR = 9


def kernel(
    nh, act, kmat, vmat, queries, order, out,
    act_v, wraw, w, acc, kv, qbuf, kpos, qpos, mold, lold, aold, oout, oin, sout, sin, fin,
    lsem, wsend, wrecv, zsend, krecv, ysend, csend, qsend, qrecv, osend, orecv, ssend, srecv, asend, arecv,
):
    head = lax.axis_index("head")
    inner = lax.axis_index("inner")
    outer = lax.axis_index("outer")
    y, c = lax.div(head, 2), lax.rem(head, 2)
    k, x = lax.div(inner, NX), lax.rem(inner, NX)
    z = k * 4 + outer
    group = lax.div(y, 2)
    side = lax.rem(y, 2)

    def at_z(step):
        return lax.rem(z + step + NZ, NZ)

    def at_x(step):
        return lax.rem(x + step + NX, NX)

    def at_k(step):
        return lax.rem(k + step + 4, 4)

    def dev_xz(px, pz):
        return (head, lax.div(pz, 4) * NX + px, lax.rem(pz, 4))

    def dev_h(h):
        return (h, inner, outer)

    y_mate = dev_h((y + 1 - 2 * side) * 2 + c)
    c_mate = dev_h(y * 2 + 1 - c)
    y_cross = dev_h((y + 1 - 2 * side) * 2 + 1 - c)

    sin[...] = jnp.zeros_like(sin)

    barrier = pltpu.get_barrier_semaphore()
    peers = [dev_xz(x, at_z(s)) for s in (-4, 4, -3, 3, -2, 2, -1, 1)]
    peers += [dev_xz(at_x(s), z) for s in (1, 2, 3)]
    for p in peers:
        pl.semaphore_signal(barrier, inc=1, device_id=p, device_id_type=MESH)

    def greet(s, carry):
        pl.semaphore_signal(barrier, inc=1, device_id=dev_h(lax.rem(head + s, nh)), device_id_type=MESH)
        return carry

    lax.fori_loop(1, nh, greet, 0)

    def load(src, dst, n):
        cp = pltpu.make_async_copy(src, dst, lsem.at[n])
        cp.start()
        return cp

    cols = pl.ds(pl.multiple_of(group * D, D), D)

    @pl.when(side == 0)
    def _():
        load(kmat.at[:, cols], wraw, 0)

    @pl.when(side == 1)
    def _():
        load(vmat.at[:, cols], wraw, 0)

    act_cp = load(act, act_v, 1)
    q_cp = load(queries, qbuf.at[x], 2)

    pltpu.make_async_copy(kmat.at[:, cols], wraw, lsem.at[0]).wait()
    lane = lax.broadcasted_iota(jnp.int32, (256, D), 1)
    left = lane < BLK
    top, bottom = wraw[0:256, :].astype(F32), wraw[256:512, :].astype(F32)
    direct = jnp.where(left, top, bottom)
    rolled = jnp.where(left, pltpu.roll(top, BLK, 1), pltpu.roll(bottom, BLK, 1))
    straight = (lane >= BLK).astype(jnp.int32) == jnp.full((256, D), c, jnp.int32)
    w[k, x] = jnp.where(straight, direct, rolled).astype(BF)

    pl.semaphore_wait(barrier, len(peers) + nh - 1)

    started = []

    def wcopy(bk, bx, half, n, device):
        part = w.at[bk, bx, pl.ds(half * 128, 128)]
        return pltpu.make_async_remote_copy(
            part, part, wsend.at[n], wrecv.at[bk, bx, half], device_id=device, device_id_type=MESH
        )

    def wput(bk, bx, half, device):
        cp = wcopy(bk, bx, half, len(started), device)
        started.append(cp)
        cp.start()

    def wgot(bk, bx, half):
        wcopy(bk, bx, half, 0, c_mate).wait_recv()

    right, left_z = dev_xz(x, at_z(4)), dev_xz(x, at_z(-4))
    ku, kd, ko = at_k(1), at_k(-1), at_k(2)
    others = [dev_xz(at_x(s), z) for s in (2, 1, 3)]

    def spread(bk, half):
        for device in others:
            wput(bk, x, half, device)

    wput(k, x, 0, right)
    wput(k, x, 1, left_z)
    wput(k, x, 1, right)
    wput(k, x, 0, left_z)
    spread(k, 0)
    spread(k, 1)

    lanes = lax.broadcasted_iota(jnp.int32, (1, D), 1)
    for slot, offset in enumerate(ARRIVE):
        zz = at_z(offset)
        first = ((lax.div(zz, 4) * NX + x) * 4 + lax.rem(zz, 4)) * 2
        b0, b1 = order[first], order[first + 1]
        kpos[0:1, slot * TOK : (slot + 1) * TOK] = jnp.where(
            lanes < BLK, b0 * BLK + lanes, b1 * BLK + lanes - BLK
        )
    rows = lax.broadcasted_iota(jnp.int32, (TOK, D), 0)
    for xx in range(NX):
        first = ((k * NX + xx) * 4 + outer) * 2
        b0, b1 = order[first], order[first + 1]
        qpos[xx] = jnp.where(rows < BLK, b0 * BLK + rows, b1 * BLK + rows - BLK)

    act_cp.wait()
    acc[...] = jnp.zeros_like(acc)

    def project(bk, bx):
        base = (bk * NX + bx) * 512
        for i in range(2):
            rows_of = act_v[:, pl.ds(pl.multiple_of(base + i * 256, 256), 256)]
            acc[i] += jnp.dot(rows_of, w[bk, bx], preferred_element_type=F32)

    project(k, x)

    wgot(kd, x, 0)
    wput(kd, x, 0, right)
    spread(kd, 0)
    wgot(ku, x, 1)
    wput(ku, x, 1, left_z)
    spread(ku, 1)
    wgot(kd, x, 1)
    spread(kd, 1)
    wgot(ku, x, 0)
    spread(ku, 0)

    def rest(bk):
        for step in (1, 3, 2):
            bx = at_x(step)
            wgot(bk, bx, 0)
            wgot(bk, bx, 1)
            project(bk, bx)

    rest(k)
    for half in range(2):
        wgot(ko, x, half)
        spread(ko, half)
    q_cp.wait()
    q_sent = []
    for i, s in enumerate((2, 1, 3)):
        cp = pltpu.make_async_remote_copy(
            qbuf.at[x], qbuf.at[x], qsend.at[i], qrecv.at[x],
            device_id=dev_xz(at_x(s), z), device_id_type=MESH,
        )
        cp.start()
        q_sent.append(cp)

    for bk in (kd, ku, ko):
        project(bk, x)
    for bk in (kd, ku, ko):
        rest(bk)

    product = acc[0] + pltpu.roll(acc[1], BLK, 1)
    own = pl.ds(pl.multiple_of(c * BLK, BLK), BLK)
    kv[side, own, 0:TOK] = product.T[0:BLK, :].astype(BF)

    def piece(sd, cc, slot, lo=0, n=BLK):
        columns = slot * TOK if isinstance(slot, int) else pl.multiple_of(slot * TOK, TOK)
        return kv.at[sd, pl.ds(pl.multiple_of(cc * BLK + lo, 32), n), pl.ds(columns, TOK)]

    def kcopy(sd, cc, slot, send, device, to=None, lo=0, n=BLK):
        to = slot if to is None else to
        return pltpu.make_async_remote_copy(
            piece(sd, cc, slot, lo, n), piece(sd, cc, to, lo, n), send, krecv.at[sd, cc, to],
            device_id=device, device_id_type=MESH,
        )

    zsent = []

    def zput(offset, step, lo=0, n=BLK):
        to = SLOT[(offset - step) % NZ]
        cp = kcopy(side, c, SLOT[offset % NZ], zsend.at[len(zsent)], dev_xz(x, at_z(step)), to, lo, n)
        zsent.append(cp)
        cp.start()

    def kgot(sd, cc, slot):
        kcopy(sd, cc, slot, zsend.at[0], c_mate).wait_recv()

    def to_mates(slot):
        kcopy(side, c, slot, ysend.at[slot], y_mate).start()
        kcopy(side, c, slot, csend.at[0, slot], c_mate).start()
        if slot >= NEAR:
            kcopy(side, c, slot, csend.at[1, slot], y_cross).start()

    def relay(slot):
        kgot(1 - side, c, slot)
        kcopy(1 - side, c, slot, csend.at[1, slot], c_mate).start()

    def take(slot):
        kgot(side, c, slot)
        to_mates(slot)

    zput(0, 4)
    zput(0, -4)
    to_mates(0)
    for s in (3, -3, 2, -2, 1, -1):
        zput(0, s)
    kgot(side, c, SLOT[12])
    zput(-4, 4, 0, 32)
    for s in (3, 2, 1):
        zput(-4, s)
    kgot(side, c, SLOT[4])
    zput(4, -4, 32, 32)
    for s in (-3, -2, -1):
        zput(4, s)
    to_mates(SLOT[12])
    to_mates(SLOT[4])
    for slot in range(1, 7):
        take(slot)
    for turn in range(3):
        take(NEAR + 2 * turn)
        take(NEAR + 2 * turn + 1)
        for slot in range(3 * turn, 3 * turn + 3):
            relay(slot)
    take(NZ - 1)
    for s in (2, 1, 3):
        pltpu.make_async_remote_copy(
            qbuf.at[x], qbuf.at[at_x(s)], qsend.at[0], qrecv.at[at_x(s)], device_id=c_mate, device_id_type=MESH
        ).wait_recv()
    for slot in range(NEAR):
        kgot(side, 1 - c, slot)
        kgot(1 - side, 1 - c, slot)

    factor = math.log2(math.e) / math.sqrt(D)
    stat_lane = lax.broadcasted_iota(jnp.int32, (TOK, D), 1)
    near, far = pl.ds(0, NEAR * TOK), pl.ds(NEAR * TOK, (NZ - NEAR) * TOK)

    def scores(xq, part):
        s = jnp.dot(both_heads(xq), kv[0, :, part], preferred_element_type=F32)
        allowed = kpos[0:1, part] <= qpos[xq][:, 0:1]
        return jnp.where(allowed[None], s.reshape(2, TOK, -1), LOW).reshape(s.shape)

    def mix(p, part):
        return lax.dot_general(
            p.astype(BF), kv[1, :, part], (((1,), (1,)), ((), ())), preferred_element_type=F32
        )

    def both_heads(xq):
        return jnp.concatenate([qbuf[xq, :, 0:D], qbuf[xq, :, D : 2 * D]], axis=0)

    def first_part(i, carry):
        xq = lax.rem(x + 3 - i, NX)
        s = scores(xq, near)
        m = jnp.maximum(jnp.max(s, axis=1, keepdims=True), FLOOR)
        p = jnp.exp2((s - m) * factor)
        mold[i] = jnp.broadcast_to(m, (2 * TOK, D))
        lold[i] = jnp.broadcast_to(jnp.sum(p, axis=1, keepdims=True), (2 * TOK, D))
        aold[i] = mix(p, near)
        return carry

    lax.fori_loop(0, NX, first_part, 0)
    for slot in range(NEAR, NZ):
        kgot(1 - side, c, slot)
        kgot(side, 1 - c, slot)
        kgot(1 - side, 1 - c, slot)

    def ocopy(xq, xs, i, device):
        return (
            pltpu.make_async_remote_copy(
                oout.at[xq], oin.at[xs], osend.at[i], orecv.at[xs], device_id=device, device_id_type=MESH
            ),
            pltpu.make_async_remote_copy(
                sout.at[xq], sin.at[pl.ds(pl.multiple_of(xs * 8, 8), 8)], ssend.at[i], srecv.at[xs],
                device_id=device, device_id_type=MESH,
            ),
        )

    def second_part(i, carry):
        xq = lax.rem(x + 3 - i, NX)
        s = scores(xq, far)
        before = mold[i][:, 0:1]
        m = jnp.maximum(jnp.max(s, axis=1, keepdims=True), before)
        p = jnp.exp2((s - m) * factor)
        fade = jnp.exp2((before - m) * factor)
        total = lold[i][:, 0:1] * fade + jnp.sum(p, axis=1, keepdims=True)
        o = ((aold[i] * fade + mix(p, far)) / jnp.maximum(total, 1e-30)).astype(BF)
        stats = jnp.zeros((TOK, D), F32)
        for hh in range(2):
            rows_of = slice(hh * TOK, (hh + 1) * TOK)
            oout[xq, :, hh * D : (hh + 1) * D] = o[rows_of]
            stats = jnp.where(stat_lane == 2 * hh, m[rows_of], stats)
            stats = jnp.where(stat_lane == 2 * hh + 1, total[rows_of], stats)
        sout[xq] = stats.T[0:8, :]

        @pl.when(i < NX - 1)
        def _():
            for cp in ocopy(xq, x, i, dev_xz(xq, z)):
                cp.start()

        return carry

    lax.fori_loop(0, NX, second_part, 0)
    for s in (1, 3, 2):
        for cp in ocopy(at_x(s), at_x(s), 0, c_mate):
            cp.wait_recv()
    oin[x] = oout[x]
    sin[pl.ds(pl.multiple_of(x * 8, 8), 8), :] = sout[x]

    st = sin[...].T
    for hh in range(2):
        ms = [st[:, 8 * i + 2 * hh : 8 * i + 2 * hh + 1] for i in range(NX)]
        ls = [st[:, 8 * i + 2 * hh + 1 : 8 * i + 2 * hh + 2] for i in range(NX)]
        top_m = functools.reduce(jnp.maximum, ms)
        ws = [l * jnp.exp2((m - top_m) * factor) for m, l in zip(ms, ls)]
        denom = functools.reduce(jnp.add, ws)
        mixed = functools.reduce(
            jnp.add,
            [(wt / denom) * oin[i, :, hh * D : (hh + 1) * D].astype(F32) for i, wt in enumerate(ws)],
        )
        fin[:, :, hh * D : (hh + 1) * D] = mixed.reshape(TOK // 8, 8, D).astype(BF)

    def acopy(j, h, i, device):
        return pltpu.make_async_remote_copy(
            fin.at[j], out.at[:, pl.ds(pl.multiple_of(h * 2 * D, 2 * D), 2 * D)],
            asend.at[i], arecv.at[h], device_id=device, device_id_type=MESH,
        )

    def scatter(i, carry):
        s = lax.rem(i + nh // 4, nh - 1) + 1
        j = lax.rem(head + s, nh)
        acopy(j, head, s, dev_h(j)).start()
        return carry

    lax.fori_loop(1, nh, scatter, 0)
    own_rows = load(fin.at[head], out.at[:, pl.ds(pl.multiple_of(head * 2 * D, 2 * D), 2 * D)], 0)
    own_rows.wait()

    for cp in started + q_sent + zsent:
        cp.wait_send()
    for slot in range(NZ):
        kcopy(side, c, slot, ysend.at[slot], y_mate).wait_send()
        kcopy(side, c, slot, csend.at[0, slot], c_mate).wait_send()
        kcopy(side, c, slot, csend.at[1, slot], c_mate).wait_send()
    for i in range(NX - 1):
        xq = lax.rem(x + 3 - i, NX)
        for cp in ocopy(xq, x, i, dev_xz(xq, z)):
            cp.wait_send()

    def close(s, carry):
        j = lax.rem(head + s, nh)
        cp = acopy(j, j, s, dev_h(j))
        cp.wait_send()
        cp.wait_recv()
        return carry

    lax.fori_loop(1, nh, close, 0)


def layer(nh, activations, key_matrix, value_matrix, queries, block_order):
    dma = pltpu.SemaphoreType.DMA
    stays = pl.BlockSpec(memory_space=pltpu.HBM)
    result = pl.pallas_call(
        functools.partial(kernel, nh),
        out_shape=jax.ShapeDtypeStruct((8, nh * 2 * D), BF),
        in_specs=[stays] * 4 + [pl.BlockSpec(memory_space=pltpu.SMEM)],
        out_specs=stays,
        scratch_shapes=[
            pltpu.VMEM((TOK, 8192), BF),
            pltpu.VMEM((512, D), BF),
            pltpu.VMEM((4, NX, 256, D), BF),
            pltpu.VMEM((2, TOK, D), F32),
            pltpu.VMEM((2, D, NZ * TOK), BF),
            pltpu.VMEM((NX, TOK, 2 * D), BF),
            pltpu.VMEM((8, NZ * TOK), jnp.int32),
            pltpu.VMEM((NX, TOK, D), jnp.int32),
            pltpu.VMEM((NX, 2 * TOK, D), F32),
            pltpu.VMEM((NX, 2 * TOK, D), F32),
            pltpu.VMEM((NX, 2 * TOK, D), F32),
            pltpu.VMEM((NX, TOK, 2 * D), BF),
            pltpu.VMEM((NX, TOK, 2 * D), BF),
            pltpu.VMEM((NX, 8, D), F32),
            pltpu.VMEM((D, D), F32),
            pltpu.VMEM((TOK // 8, 8, 2 * D), BF),
            dma((3,)),
            dma((30,)),
            dma((4, NX, 2)),
            dma((16,)),
            dma((2, 2, NZ)),
            dma((NZ,)),
            dma((2, NZ)),
            dma((3,)),
            dma((NX,)),
            dma((NX,)),
            dma((NX,)),
            dma((NX,)),
            dma((NX,)),
            dma((nh,)),
            dma((nh,)),
        ],
        compiler_params=pltpu.CompilerParams(collective_id=0, has_side_effects=True),
    )(activations, key_matrix, value_matrix, queries, block_order)
    return result.reshape(1, 1, 8, nh * 2 * D)


def solution(mesh):
    placed = (
        P(("inner", "outer"), None),
        P("inner", None),
        P("inner", None),
        P(("inner", "outer"), "head"),
        P(),
    )
    return jax.shard_map(
        functools.partial(layer, mesh.shape["head"]),
        mesh=mesh,
        in_specs=placed,
        out_specs=P(("inner", "outer"), "head", None, None),
        check_vma=False,
    )
```

```python
import functools
import math

import jax
import jax.numpy as jnp
from jax import lax
from jax.experimental import pallas as pl
from jax.experimental.pallas import tpu as pltpu
from jax.sharding import PartitionSpec as P

D = 128
TOK = 128
BLK = 64
NX = 4
NZ = 16
LOW = -1e30
FLOOR = -1e28
MESH = pl.DeviceIdType.MESH
BF = jnp.bfloat16
F32 = jnp.float32
ARRIVE = (0, 15, 1, 14, 2, 13, 3, 12, 4, 11, 5, 10, 6, 9, 7, 8)
SLOT = {offset: slot for slot, offset in enumerate(ARRIVE)}
NEAR = 9


def kernel(
    nh, act, kmat, vmat, queries, order, out,
    act_v, wraw, w, acc, kv, qbuf, kpos, qpos, mold, lold, aold, oout, oin, sout, sin, fin,
    lsem, wsend, wrecv, zsend, krecv, ysend, csend, qsend, qrecv, osend, orecv, ssend, srecv, asend, arecv,
):
    head = lax.axis_index("head")
    inner = lax.axis_index("inner")
    outer = lax.axis_index("outer")
    y, c = lax.div(head, 2), lax.rem(head, 2)
    k, x = lax.div(inner, NX), lax.rem(inner, NX)
    z = k * 4 + outer
    group = lax.div(y, 2)
    side = lax.rem(y, 2)

    def at_z(step):
        return lax.rem(z + step + NZ, NZ)

    def at_x(step):
        return lax.rem(x + step + NX, NX)

    def at_k(step):
        return lax.rem(k + step + 4, 4)

    def dev_xz(px, pz):
        return (head, lax.div(pz, 4) * NX + px, lax.rem(pz, 4))

    def dev_h(h):
        return (h, inner, outer)

    y_mate = dev_h((y + 1 - 2 * side) * 2 + c)
    c_mate = dev_h(y * 2 + 1 - c)
    y_cross = dev_h((y + 1 - 2 * side) * 2 + 1 - c)

    sin[...] = jnp.zeros_like(sin)

    barrier = pltpu.get_barrier_semaphore()
    peers = [dev_xz(x, at_z(s)) for s in (-4, 4, -3, 3, -2, 2, -1, 1)]
    peers += [dev_xz(at_x(s), z) for s in (1, 2, 3)]
    for p in peers:
        pl.semaphore_signal(barrier, inc=1, device_id=p, device_id_type=MESH)

    def greet(s, carry):
        pl.semaphore_signal(barrier, inc=1, device_id=dev_h(lax.rem(head + s, nh)), device_id_type=MESH)
        return carry

    lax.fori_loop(1, nh, greet, 0)

    def load(src, dst, n):
        cp = pltpu.make_async_copy(src, dst, lsem.at[n])
        cp.start()
        return cp

    cols = pl.ds(pl.multiple_of(group * D, D), D)

    @pl.when(side == 0)
    def _():
        load(kmat.at[:, cols], wraw, 0)

    @pl.when(side == 1)
    def _():
        load(vmat.at[:, cols], wraw, 0)

    act_cp = load(act, act_v, 1)
    q_cp = load(queries, qbuf.at[x], 2)

    pltpu.make_async_copy(kmat.at[:, cols], wraw, lsem.at[0]).wait()
    lane = lax.broadcasted_iota(jnp.int32, (256, D), 1)
    left = lane < BLK
    top, bottom = wraw[0:256, :].astype(F32), wraw[256:512, :].astype(F32)
    direct = jnp.where(left, top, bottom)
    rolled = jnp.where(left, pltpu.roll(top, BLK, 1), pltpu.roll(bottom, BLK, 1))
    straight = (lane >= BLK).astype(jnp.int32) == jnp.full((256, D), c, jnp.int32)
    w[k, x] = jnp.where(straight, direct, rolled).astype(BF)

    pl.semaphore_wait(barrier, len(peers) + nh - 1)

    started = []

    def wcopy(bk, bx, half, n, device):
        part = w.at[bk, bx, pl.ds(half * 128, 128)]
        return pltpu.make_async_remote_copy(
            part, part, wsend.at[n], wrecv.at[bk, bx, half], device_id=device, device_id_type=MESH
        )

    def wput(bk, bx, half, device):
        cp = wcopy(bk, bx, half, len(started), device)
        started.append(cp)
        cp.start()

    def wgot(bk, bx, half):
        wcopy(bk, bx, half, 0, c_mate).wait_recv()

    right, left_z = dev_xz(x, at_z(4)), dev_xz(x, at_z(-4))
    ku, kd, ko = at_k(1), at_k(-1), at_k(2)
    others = [dev_xz(at_x(s), z) for s in (2, 1, 3)]

    def spread(bk, half):
        for device in others:
            wput(bk, x, half, device)

    wput(k, x, 0, right)
    wput(k, x, 1, left_z)
    wput(k, x, 1, right)
    wput(k, x, 0, left_z)
    spread(k, 0)
    spread(k, 1)

    lanes = lax.broadcasted_iota(jnp.int32, (1, D), 1)
    for slot, offset in enumerate(ARRIVE):
        zz = at_z(offset)
        first = ((lax.div(zz, 4) * NX + x) * 4 + lax.rem(zz, 4)) * 2
        b0, b1 = order[first], order[first + 1]
        kpos[0:1, slot * TOK : (slot + 1) * TOK] = jnp.where(
            lanes < BLK, b0 * BLK + lanes, b1 * BLK + lanes - BLK
        )
    rows = lax.broadcasted_iota(jnp.int32, (TOK, D), 0)
    for xx in range(NX):
        first = ((k * NX + xx) * 4 + outer) * 2
        b0, b1 = order[first], order[first + 1]
        qpos[xx] = jnp.where(rows < BLK, b0 * BLK + rows, b1 * BLK + rows - BLK)

    act_cp.wait()
    acc[...] = jnp.zeros_like(acc)

    def project(bk, bx):
        base = (bk * NX + bx) * 512
        for i in range(2):
            rows_of = act_v[:, pl.ds(pl.multiple_of(base + i * 256, 256), 256)]
            acc[i] += jnp.dot(rows_of, w[bk, bx], preferred_element_type=F32)

    project(k, x)

    wgot(kd, x, 0)
    wput(kd, x, 0, right)
    spread(kd, 0)
    wgot(ku, x, 1)
    wput(ku, x, 1, left_z)
    spread(ku, 1)
    wgot(kd, x, 1)
    spread(kd, 1)
    wgot(ku, x, 0)
    spread(ku, 0)

    def rest(bk):
        for step in (1, 3, 2):
            bx = at_x(step)
            wgot(bk, bx, 0)
            wgot(bk, bx, 1)
            project(bk, bx)

    rest(k)
    for half in range(2):
        wgot(ko, x, half)
        spread(ko, half)
    for bk in (kd, ku, ko):
        project(bk, x)
    for bk in (kd, ku, ko):
        rest(bk)

    product = acc[0] + pltpu.roll(acc[1], BLK, 1)
    own = pl.ds(pl.multiple_of(c * BLK, BLK), BLK)
    kv[side, own, 0:TOK] = product.T[0:BLK, :].astype(BF)

    def piece(sd, cc, slot, lo=0, n=BLK):
        columns = slot * TOK if isinstance(slot, int) else pl.multiple_of(slot * TOK, TOK)
        return kv.at[sd, pl.ds(pl.multiple_of(cc * BLK + lo, 32), n), pl.ds(columns, TOK)]

    def kcopy(sd, cc, slot, send, device, to=None, lo=0, n=BLK):
        to = slot if to is None else to
        return pltpu.make_async_remote_copy(
            piece(sd, cc, slot, lo, n), piece(sd, cc, to, lo, n), send, krecv.at[sd, cc, to],
            device_id=device, device_id_type=MESH,
        )

    zsent = []

    def zput(offset, step, lo=0, n=BLK):
        to = SLOT[(offset - step) % NZ]
        cp = kcopy(side, c, SLOT[offset % NZ], zsend.at[len(zsent)], dev_xz(x, at_z(step)), to, lo, n)
        zsent.append(cp)
        cp.start()

    def kgot(sd, cc, slot):
        kcopy(sd, cc, slot, zsend.at[0], c_mate).wait_recv()

    def to_mates(slot):
        kcopy(side, c, slot, ysend.at[slot], y_mate).start()
        kcopy(side, c, slot, csend.at[0, slot], c_mate).start()
        if slot >= NEAR:
            kcopy(side, c, slot, csend.at[1, slot], y_cross).start()

    def relay(slot):
        kgot(1 - side, c, slot)
        kcopy(1 - side, c, slot, csend.at[1, slot], c_mate).start()

    def take(slot):
        kgot(side, c, slot)
        to_mates(slot)

    zput(0, 4)
    zput(0, -4)
    to_mates(0)
    for s in (3, -3, 2, -2, 1, -1):
        zput(0, s)

    q_cp.wait()
    q_sent = []
    for i, s in enumerate((2, 1, 3)):
        cp = pltpu.make_async_remote_copy(
            qbuf.at[x], qbuf.at[x], qsend.at[i], qrecv.at[x],
            device_id=dev_xz(at_x(s), z), device_id_type=MESH,
        )
        cp.start()
        q_sent.append(cp)

    kgot(side, c, SLOT[12])
    zput(-4, 4, 0, 32)
    for s in (3, 2, 1):
        zput(-4, s)
    kgot(side, c, SLOT[4])
    zput(4, -4, 32, 32)
    for s in (-3, -2, -1):
        zput(4, s)
    to_mates(SLOT[12])
    to_mates(SLOT[4])
    for slot in range(1, 7):
        take(slot)
    for turn in range(3):
        take(NEAR + 2 * turn)
        take(NEAR + 2 * turn + 1)
        for slot in range(3 * turn, 3 * turn + 3):
            relay(slot)
    take(NZ - 1)
    for s in (2, 1, 3):
        pltpu.make_async_remote_copy(
            qbuf.at[x], qbuf.at[at_x(s)], qsend.at[0], qrecv.at[at_x(s)], device_id=c_mate, device_id_type=MESH
        ).wait_recv()
    for slot in range(NEAR):
        kgot(side, 1 - c, slot)
        kgot(1 - side, 1 - c, slot)

    factor = math.log2(math.e) / math.sqrt(D)
    stat_lane = lax.broadcasted_iota(jnp.int32, (TOK, D), 1)
    near, far = pl.ds(0, NEAR * TOK), pl.ds(NEAR * TOK, (NZ - NEAR) * TOK)

    def scores(xq, part):
        s = jnp.dot(both_heads(xq), kv[0, :, part], preferred_element_type=F32)
        allowed = kpos[0:1, part] <= qpos[xq][:, 0:1]
        return jnp.where(allowed[None], s.reshape(2, TOK, -1), LOW).reshape(s.shape)

    def mix(p, part):
        return lax.dot_general(
            p.astype(BF), kv[1, :, part], (((1,), (1,)), ((), ())), preferred_element_type=F32
        )

    def both_heads(xq):
        return jnp.concatenate([qbuf[xq, :, 0:D], qbuf[xq, :, D : 2 * D]], axis=0)

    def first_part(i, carry):
        xq = lax.rem(x + 3 - i, NX)
        s = scores(xq, near)
        m = jnp.maximum(jnp.max(s, axis=1, keepdims=True), FLOOR)
        p = jnp.exp2((s - m) * factor)
        mold[i] = jnp.broadcast_to(m, (2 * TOK, D))
        lold[i] = jnp.broadcast_to(jnp.sum(p, axis=1, keepdims=True), (2 * TOK, D))
        aold[i] = mix(p, near)
        return carry

    lax.fori_loop(0, NX, first_part, 0, unroll=True)
    for slot in range(NEAR, NZ):
        kgot(1 - side, c, slot)
        kgot(side, 1 - c, slot)
        kgot(1 - side, 1 - c, slot)

    def ocopy(xq, xs, i, device):
        return (
            pltpu.make_async_remote_copy(
                oout.at[xq], oin.at[xs], osend.at[i], orecv.at[xs], device_id=device, device_id_type=MESH
            ),
            pltpu.make_async_remote_copy(
                sout.at[xq], sin.at[pl.ds(pl.multiple_of(xs * 8, 8), 8)], ssend.at[i], srecv.at[xs],
                device_id=device, device_id_type=MESH,
            ),
        )

    def second_part(i, carry):
        xq = lax.rem(x + 3 - i, NX)
        s = scores(xq, far)
        before = mold[i][:, 0:1]
        m = jnp.maximum(jnp.max(s, axis=1, keepdims=True), before)
        p = jnp.exp2((s - m) * factor)
        fade = jnp.exp2((before - m) * factor)
        total = lold[i][:, 0:1] * fade + jnp.sum(p, axis=1, keepdims=True)
        o = ((aold[i] * fade + mix(p, far)) / jnp.maximum(total, 1e-30)).astype(BF)
        stats = jnp.zeros((TOK, D), F32)
        for hh in range(2):
            rows_of = slice(hh * TOK, (hh + 1) * TOK)
            oout[xq, :, hh * D : (hh + 1) * D] = o[rows_of]
            stats = jnp.where(stat_lane == 2 * hh, m[rows_of], stats)
            stats = jnp.where(stat_lane == 2 * hh + 1, total[rows_of], stats)
        sout[xq] = stats.T[0:8, :]

        @pl.when(i < NX - 1)
        def _():
            for cp in ocopy(xq, x, i, dev_xz(xq, z)):
                cp.start()

        return carry

    lax.fori_loop(0, NX, second_part, 0)
    for s in (1, 3, 2):
        for cp in ocopy(at_x(s), at_x(s), 0, c_mate):
            cp.wait_recv()
    oin[x] = oout[x]
    sin[pl.ds(pl.multiple_of(x * 8, 8), 8), :] = sout[x]

    st = sin[...].T
    for hh in range(2):
        ms = [st[:, 8 * i + 2 * hh : 8 * i + 2 * hh + 1] for i in range(NX)]
        ls = [st[:, 8 * i + 2 * hh + 1 : 8 * i + 2 * hh + 2] for i in range(NX)]
        top_m = functools.reduce(jnp.maximum, ms)
        ws = [l * jnp.exp2((m - top_m) * factor) for m, l in zip(ms, ls)]
        denom = functools.reduce(jnp.add, ws)
        mixed = functools.reduce(
            jnp.add,
            [(wt / denom) * oin[i, :, hh * D : (hh + 1) * D].astype(F32) for i, wt in enumerate(ws)],
        )
        fin[:, :, hh * D : (hh + 1) * D] = mixed.reshape(TOK // 8, 8, D).astype(BF)

    def acopy(j, h, i, device):
        return pltpu.make_async_remote_copy(
            fin.at[j], out.at[:, pl.ds(pl.multiple_of(h * 2 * D, 2 * D), 2 * D)],
            asend.at[i], arecv.at[h], device_id=device, device_id_type=MESH,
        )

    def scatter(i, carry):
        s = lax.rem(i + nh // 4, nh - 1) + 1
        j = lax.rem(head + s, nh)
        acopy(j, head, s, dev_h(j)).start()
        return carry

    lax.fori_loop(1, nh, scatter, 0)
    own_rows = load(fin.at[head], out.at[:, pl.ds(pl.multiple_of(head * 2 * D, 2 * D), 2 * D)], 0)
    own_rows.wait()

    for cp in started + q_sent + zsent:
        cp.wait_send()
    for slot in range(NZ):
        kcopy(side, c, slot, ysend.at[slot], y_mate).wait_send()
        kcopy(side, c, slot, csend.at[0, slot], c_mate).wait_send()
        kcopy(side, c, slot, csend.at[1, slot], c_mate).wait_send()
    for i in range(NX - 1):
        xq = lax.rem(x + 3 - i, NX)
        for cp in ocopy(xq, x, i, dev_xz(xq, z)):
            cp.wait_send()

    def close(s, carry):
        j = lax.rem(head + s, nh)
        cp = acopy(j, j, s, dev_h(j))
        cp.wait_send()
        cp.wait_recv()
        return carry

    lax.fori_loop(1, nh, close, 0)


def layer(nh, activations, key_matrix, value_matrix, queries, block_order):
    dma = pltpu.SemaphoreType.DMA
    stays = pl.BlockSpec(memory_space=pltpu.HBM)
    result = pl.pallas_call(
        functools.partial(kernel, nh),
        out_shape=jax.ShapeDtypeStruct((8, nh * 2 * D), BF),
        in_specs=[stays] * 4 + [pl.BlockSpec(memory_space=pltpu.SMEM)],
        out_specs=stays,
        scratch_shapes=[
            pltpu.VMEM((TOK, 8192), BF),
            pltpu.VMEM((512, D), BF),
            pltpu.VMEM((4, NX, 256, D), BF),
            pltpu.VMEM((2, TOK, D), F32),
            pltpu.VMEM((2, D, NZ * TOK), BF),
            pltpu.VMEM((NX, TOK, 2 * D), BF),
            pltpu.VMEM((8, NZ * TOK), jnp.int32),
            pltpu.VMEM((NX, TOK, D), jnp.int32),
            pltpu.VMEM((NX, 2 * TOK, D), F32),
            pltpu.VMEM((NX, 2 * TOK, D), F32),
            pltpu.VMEM((NX, 2 * TOK, D), F32),
            pltpu.VMEM((NX, TOK, 2 * D), BF),
            pltpu.VMEM((NX, TOK, 2 * D), BF),
            pltpu.VMEM((NX, 8, D), F32),
            pltpu.VMEM((D, D), F32),
            pltpu.VMEM((TOK // 8, 8, 2 * D), BF),
            dma((3,)),
            dma((30,)),
            dma((4, NX, 2)),
            dma((16,)),
            dma((2, 2, NZ)),
            dma((NZ,)),
            dma((2, NZ)),
            dma((3,)),
            dma((NX,)),
            dma((NX,)),
            dma((NX,)),
            dma((NX,)),
            dma((NX,)),
            dma((nh,)),
            dma((nh,)),
        ],
        compiler_params=pltpu.CompilerParams(collective_id=0, has_side_effects=True),
    )(activations, key_matrix, value_matrix, queries, block_order)
    return result.reshape(1, 1, 8, nh * 2 * D)


def solution(mesh):
    placed = (
        P(("inner", "outer"), None),
        P("inner", None),
        P("inner", None),
        P(("inner", "outer"), "head"),
        P(),
    )
    return jax.shard_map(
        functools.partial(layer, mesh.shape["head"]),
        mesh=mesh,
        in_specs=placed,
        out_specs=P(("inner", "outer"), "head", None, None),
        check_vma=False,
    )
```

```python
import functools
import math

import jax
import jax.numpy as jnp
from jax import lax
from jax.experimental import pallas as pl
from jax.experimental.pallas import tpu as pltpu
from jax.sharding import PartitionSpec as P

D = 128
TOK = 128
BLK = 64
NX = 4
NZ = 16
LOW = -1e30
FLOOR = -1e28
MESH = pl.DeviceIdType.MESH
BF = jnp.bfloat16
F32 = jnp.float32
ARRIVE = (0, 15, 1, 14, 2, 13, 3, 12, 4, 11, 5, 10, 6, 9, 7, 8)
SLOT = {offset: slot for slot, offset in enumerate(ARRIVE)}
NEAR = 9
CROSS = 5


def kernel(
    nh, act, kmat, vmat, queries, order, out,
    act_v, wraw, w, acc, kv, qbuf, kpos, qpos, mold, lold, aold, oout, oin, sout, sin, fin,
    lsem, wsend, wrecv, zsend, krecv, ysend, csend, qsend, qrecv, osend, orecv, ssend, srecv, asend, arecv,
):
    head = lax.axis_index("head")
    inner = lax.axis_index("inner")
    outer = lax.axis_index("outer")
    y, c = lax.div(head, 2), lax.rem(head, 2)
    k, x = lax.div(inner, NX), lax.rem(inner, NX)
    z = k * 4 + outer
    group = lax.div(y, 2)
    side = lax.rem(y, 2)

    def at_z(step):
        return lax.rem(z + step + NZ, NZ)

    def at_x(step):
        return lax.rem(x + step + NX, NX)

    def at_k(step):
        return lax.rem(k + step + 4, 4)

    def dev_xz(px, pz):
        return (head, lax.div(pz, 4) * NX + px, lax.rem(pz, 4))

    def dev_h(h):
        return (h, inner, outer)

    y_mate = dev_h((y + 1 - 2 * side) * 2 + c)
    c_mate = dev_h(y * 2 + 1 - c)
    y_cross = dev_h((y + 1 - 2 * side) * 2 + 1 - c)

    sin[...] = jnp.zeros_like(sin)

    barrier = pltpu.get_barrier_semaphore()
    peers = [dev_xz(x, at_z(s)) for s in (-4, 4, -3, 3, -2, 2, -1, 1)]
    peers += [dev_xz(at_x(s), z) for s in (1, 2, 3)]
    for p in peers:
        pl.semaphore_signal(barrier, inc=1, device_id=p, device_id_type=MESH)

    def greet(s, carry):
        pl.semaphore_signal(barrier, inc=1, device_id=dev_h(lax.rem(head + s, nh)), device_id_type=MESH)
        return carry

    lax.fori_loop(1, nh, greet, 0)

    def load(src, dst, n):
        cp = pltpu.make_async_copy(src, dst, lsem.at[n])
        cp.start()
        return cp

    cols = pl.ds(pl.multiple_of(group * D, D), D)

    @pl.when(side == 0)
    def _():
        load(kmat.at[:, cols], wraw, 0)

    @pl.when(side == 1)
    def _():
        load(vmat.at[:, cols], wraw, 0)

    act_cp = load(act, act_v, 1)
    q_cp = load(queries, qbuf.at[x], 2)

    pltpu.make_async_copy(kmat.at[:, cols], wraw, lsem.at[0]).wait()
    lane = lax.broadcasted_iota(jnp.int32, (256, D), 1)
    left = lane < BLK
    top, bottom = wraw[0:256, :].astype(F32), wraw[256:512, :].astype(F32)
    direct = jnp.where(left, top, bottom)
    rolled = jnp.where(left, pltpu.roll(top, BLK, 1), pltpu.roll(bottom, BLK, 1))
    straight = (lane >= BLK).astype(jnp.int32) == jnp.full((256, D), c, jnp.int32)
    w[k, x] = jnp.where(straight, direct, rolled).astype(BF)

    pl.semaphore_wait(barrier, len(peers) + nh - 1)

    started = []

    def wcopy(bk, bx, half, n, device):
        part = w.at[bk, bx, pl.ds(half * 128, 128)]
        return pltpu.make_async_remote_copy(
            part, part, wsend.at[n], wrecv.at[bk, bx, half], device_id=device, device_id_type=MESH
        )

    def wput(bk, bx, half, device):
        cp = wcopy(bk, bx, half, len(started), device)
        started.append(cp)
        cp.start()

    def wgot(bk, bx, half):
        wcopy(bk, bx, half, 0, c_mate).wait_recv()

    right, left_z = dev_xz(x, at_z(4)), dev_xz(x, at_z(-4))
    ku, kd, ko = at_k(1), at_k(-1), at_k(2)
    others = [dev_xz(at_x(s), z) for s in (2, 1, 3)]

    def spread(bk, half):
        for device in others:
            wput(bk, x, half, device)

    wput(k, x, 0, right)
    wput(k, x, 1, left_z)
    wput(k, x, 1, right)
    wput(k, x, 0, left_z)
    spread(k, 0)
    spread(k, 1)

    lanes = lax.broadcasted_iota(jnp.int32, (1, D), 1)
    for slot, offset in enumerate(ARRIVE):
        zz = at_z(offset)
        first = ((lax.div(zz, 4) * NX + x) * 4 + lax.rem(zz, 4)) * 2
        b0, b1 = order[first], order[first + 1]
        kpos[0:1, slot * TOK : (slot + 1) * TOK] = jnp.where(
            lanes < BLK, b0 * BLK + lanes, b1 * BLK + lanes - BLK
        )
    rows = lax.broadcasted_iota(jnp.int32, (TOK, D), 0)
    for xx in range(NX):
        first = ((k * NX + xx) * 4 + outer) * 2
        b0, b1 = order[first], order[first + 1]
        qpos[xx] = jnp.where(rows < BLK, b0 * BLK + rows, b1 * BLK + rows - BLK)

    act_cp.wait()
    acc[...] = jnp.zeros_like(acc)

    def project(bk, bx):
        base = (bk * NX + bx) * 512
        for i in range(2):
            rows_of = act_v[:, pl.ds(pl.multiple_of(base + i * 256, 256), 256)]
            acc[i] += jnp.dot(rows_of, w[bk, bx], preferred_element_type=F32)

    project(k, x)

    wgot(kd, x, 0)
    wput(kd, x, 0, right)
    spread(kd, 0)
    wgot(ku, x, 1)
    wput(ku, x, 1, left_z)
    spread(ku, 1)
    wgot(kd, x, 1)
    spread(kd, 1)
    wgot(ku, x, 0)
    spread(ku, 0)

    def rest(bk):
        for step in (1, 3, 2):
            bx = at_x(step)
            wgot(bk, bx, 0)
            wgot(bk, bx, 1)
            project(bk, bx)

    rest(k)
    for half in range(2):
        wgot(ko, x, half)
        spread(ko, half)
    for bk in (kd, ku, ko):
        project(bk, x)
    for bk in (kd, ku, ko):
        rest(bk)

    product = acc[0] + pltpu.roll(acc[1], BLK, 1)
    own = pl.ds(pl.multiple_of(c * BLK, BLK), BLK)
    kv[side, own, 0:TOK] = product.T[0:BLK, :].astype(BF)

    def piece(sd, cc, slot, lo=0, n=BLK):
        columns = slot * TOK if isinstance(slot, int) else pl.multiple_of(slot * TOK, TOK)
        return kv.at[sd, pl.ds(pl.multiple_of(cc * BLK + lo, 32), n), pl.ds(columns, TOK)]

    def kcopy(sd, cc, slot, send, device, to=None, lo=0, n=BLK):
        to = slot if to is None else to
        return pltpu.make_async_remote_copy(
            piece(sd, cc, slot, lo, n), piece(sd, cc, to, lo, n), send, krecv.at[sd, cc, to],
            device_id=device, device_id_type=MESH,
        )

    zsent = []

    def zput(offset, step, lo=0, n=BLK):
        to = SLOT[(offset - step) % NZ]
        cp = kcopy(side, c, SLOT[offset % NZ], zsend.at[len(zsent)], dev_xz(x, at_z(step)), to, lo, n)
        zsent.append(cp)
        cp.start()

    def kgot(sd, cc, slot):
        kcopy(sd, cc, slot, zsend.at[0], c_mate).wait_recv()

    def to_mates(slot):
        kcopy(side, c, slot, ysend.at[slot], y_mate).start()
        kcopy(side, c, slot, csend.at[0, slot], c_mate).start()
        if slot >= CROSS:
            kcopy(side, c, slot, csend.at[1, slot], y_cross).start()

    def relay(slot):
        kgot(1 - side, c, slot)
        kcopy(1 - side, c, slot, csend.at[1, slot], c_mate).start()

    def take(slot):
        kgot(side, c, slot)
        to_mates(slot)

    zput(0, 4)
    zput(0, -4)
    to_mates(0)
    for s in (3, -3, 2, -2, 1, -1):
        zput(0, s)

    q_cp.wait()
    q_sent = []
    for i, s in enumerate((2, 1, 3)):
        cp = pltpu.make_async_remote_copy(
            qbuf.at[x], qbuf.at[x], qsend.at[i], qrecv.at[x],
            device_id=dev_xz(at_x(s), z), device_id_type=MESH,
        )
        cp.start()
        q_sent.append(cp)

    kgot(side, c, SLOT[12])
    zput(-4, 4, 0, 32)
    for s in (3, 2, 1):
        zput(-4, s)
    kgot(side, c, SLOT[4])
    zput(4, -4, 32, 32)
    for s in (-3, -2, -1):
        zput(4, s)
    to_mates(SLOT[12])
    to_mates(SLOT[4])
    for slot in range(1, 7):
        take(slot)
    for turn in range(3):
        take(NEAR + 2 * turn)
        take(NEAR + 2 * turn + 1)
        for slot in range(2 * turn, min(2 * turn + 2, CROSS)):
            relay(slot)
    take(NZ - 1)
    for s in (2, 1, 3):
        pltpu.make_async_remote_copy(
            qbuf.at[x], qbuf.at[at_x(s)], qsend.at[0], qrecv.at[at_x(s)], device_id=c_mate, device_id_type=MESH
        ).wait_recv()
    for slot in range(NEAR):
        if slot >= CROSS:
            kgot(1 - side, c, slot)
        kgot(side, 1 - c, slot)
        kgot(1 - side, 1 - c, slot)

    factor = math.log2(math.e) / math.sqrt(D)
    stat_lane = lax.broadcasted_iota(jnp.int32, (TOK, D), 1)
    near, far = pl.ds(0, NEAR * TOK), pl.ds(NEAR * TOK, (NZ - NEAR) * TOK)

    def scores(xq, part):
        s = jnp.dot(both_heads(xq), kv[0, :, part], preferred_element_type=F32)
        allowed = kpos[0:1, part] <= qpos[xq][:, 0:1]
        return jnp.where(allowed[None], s.reshape(2, TOK, -1), LOW).reshape(s.shape)

    def mix(p, part):
        return lax.dot_general(
            p.astype(BF), kv[1, :, part], (((1,), (1,)), ((), ())), preferred_element_type=F32
        )

    def both_heads(xq):
        return jnp.concatenate([qbuf[xq, :, 0:D], qbuf[xq, :, D : 2 * D]], axis=0)

    def first_part(i, carry):
        xq = lax.rem(x + 3 - i, NX)
        s = scores(xq, near)
        m = jnp.maximum(jnp.max(s, axis=1, keepdims=True), FLOOR)
        p = jnp.exp2((s - m) * factor)
        mold[i] = jnp.broadcast_to(m, (2 * TOK, D))
        lold[i] = jnp.broadcast_to(jnp.sum(p, axis=1, keepdims=True), (2 * TOK, D))
        aold[i] = mix(p, near)
        return carry

    lax.fori_loop(0, NX, first_part, 0, unroll=True)
    for slot in range(NEAR, NZ):
        kgot(1 - side, c, slot)
        kgot(side, 1 - c, slot)
        kgot(1 - side, 1 - c, slot)

    def ocopy(xq, xs, i, device):
        return (
            pltpu.make_async_remote_copy(
                oout.at[xq], oin.at[xs], osend.at[i], orecv.at[xs], device_id=device, device_id_type=MESH
            ),
            pltpu.make_async_remote_copy(
                sout.at[xq], sin.at[pl.ds(pl.multiple_of(xs * 8, 8), 8)], ssend.at[i], srecv.at[xs],
                device_id=device, device_id_type=MESH,
            ),
        )

    def second_part(i, carry):
        xq = lax.rem(x + 3 - i, NX)
        s = scores(xq, far)
        before = mold[i][:, 0:1]
        m = jnp.maximum(jnp.max(s, axis=1, keepdims=True), before)
        p = jnp.exp2((s - m) * factor)
        fade = jnp.exp2((before - m) * factor)
        total = lold[i][:, 0:1] * fade + jnp.sum(p, axis=1, keepdims=True)
        o = ((aold[i] * fade + mix(p, far)) / jnp.maximum(total, 1e-30)).astype(BF)
        stats = jnp.zeros((TOK, D), F32)
        for hh in range(2):
            rows_of = slice(hh * TOK, (hh + 1) * TOK)
            oout[xq, :, hh * D : (hh + 1) * D] = o[rows_of]
            stats = jnp.where(stat_lane == 2 * hh, m[rows_of], stats)
            stats = jnp.where(stat_lane == 2 * hh + 1, total[rows_of], stats)
        sout[xq] = stats.T[0:8, :]

        @pl.when(i < NX - 1)
        def _():
            for cp in ocopy(xq, x, i, dev_xz(xq, z)):
                cp.start()

        return carry

    lax.fori_loop(0, NX, second_part, 0)
    for s in (1, 3, 2):
        for cp in ocopy(at_x(s), at_x(s), 0, c_mate):
            cp.wait_recv()
    oin[x] = oout[x]
    sin[pl.ds(pl.multiple_of(x * 8, 8), 8), :] = sout[x]

    st = sin[...].T
    for hh in range(2):
        ms = [st[:, 8 * i + 2 * hh : 8 * i + 2 * hh + 1] for i in range(NX)]
        ls = [st[:, 8 * i + 2 * hh + 1 : 8 * i + 2 * hh + 2] for i in range(NX)]
        top_m = functools.reduce(jnp.maximum, ms)
        ws = [l * jnp.exp2((m - top_m) * factor) for m, l in zip(ms, ls)]
        denom = functools.reduce(jnp.add, ws)
        mixed = functools.reduce(
            jnp.add,
            [(wt / denom) * oin[i, :, hh * D : (hh + 1) * D].astype(F32) for i, wt in enumerate(ws)],
        )
        fin[:, :, hh * D : (hh + 1) * D] = mixed.reshape(TOK // 8, 8, D).astype(BF)

    def acopy(j, h, i, device):
        return pltpu.make_async_remote_copy(
            fin.at[j], out.at[:, pl.ds(pl.multiple_of(h * 2 * D, 2 * D), 2 * D)],
            asend.at[i], arecv.at[h], device_id=device, device_id_type=MESH,
        )

    def scatter(i, carry):
        s = lax.rem(i + nh // 4, nh - 1) + 1
        j = lax.rem(head + s, nh)
        acopy(j, head, s, dev_h(j)).start()
        return carry

    lax.fori_loop(1, nh, scatter, 0)
    own_rows = load(fin.at[head], out.at[:, pl.ds(pl.multiple_of(head * 2 * D, 2 * D), 2 * D)], 0)
    own_rows.wait()

    for cp in started + q_sent + zsent:
        cp.wait_send()
    for slot in range(NZ):
        kcopy(side, c, slot, ysend.at[slot], y_mate).wait_send()
        kcopy(side, c, slot, csend.at[0, slot], c_mate).wait_send()
        kcopy(side, c, slot, csend.at[1, slot], c_mate).wait_send()
    for i in range(NX - 1):
        xq = lax.rem(x + 3 - i, NX)
        for cp in ocopy(xq, x, i, dev_xz(xq, z)):
            cp.wait_send()

    def close(s, carry):
        j = lax.rem(head + s, nh)
        cp = acopy(j, j, s, dev_h(j))
        cp.wait_send()
        cp.wait_recv()
        return carry

    lax.fori_loop(1, nh, close, 0)


def layer(nh, activations, key_matrix, value_matrix, queries, block_order):
    dma = pltpu.SemaphoreType.DMA
    stays = pl.BlockSpec(memory_space=pltpu.HBM)
    result = pl.pallas_call(
        functools.partial(kernel, nh),
        out_shape=jax.ShapeDtypeStruct((8, nh * 2 * D), BF),
        in_specs=[stays] * 4 + [pl.BlockSpec(memory_space=pltpu.SMEM)],
        out_specs=stays,
        scratch_shapes=[
            pltpu.VMEM((TOK, 8192), BF),
            pltpu.VMEM((512, D), BF),
            pltpu.VMEM((4, NX, 256, D), BF),
            pltpu.VMEM((2, TOK, D), F32),
            pltpu.VMEM((2, D, NZ * TOK), BF),
            pltpu.VMEM((NX, TOK, 2 * D), BF),
            pltpu.VMEM((8, NZ * TOK), jnp.int32),
            pltpu.VMEM((NX, TOK, D), jnp.int32),
            pltpu.VMEM((NX, 2 * TOK, D), F32),
            pltpu.VMEM((NX, 2 * TOK, D), F32),
            pltpu.VMEM((NX, 2 * TOK, D), F32),
            pltpu.VMEM((NX, TOK, 2 * D), BF),
            pltpu.VMEM((NX, TOK, 2 * D), BF),
            pltpu.VMEM((NX, 8, D), F32),
            pltpu.VMEM((D, D), F32),
            pltpu.VMEM((TOK // 8, 8, 2 * D), BF),
            dma((3,)),
            dma((30,)),
            dma((4, NX, 2)),
            dma((16,)),
            dma((2, 2, NZ)),
            dma((NZ,)),
            dma((2, NZ)),
            dma((3,)),
            dma((NX,)),
            dma((NX,)),
            dma((NX,)),
            dma((NX,)),
            dma((NX,)),
            dma((nh,)),
            dma((nh,)),
        ],
        compiler_params=pltpu.CompilerParams(collective_id=0, has_side_effects=True),
    )(activations, key_matrix, value_matrix, queries, block_order)
    return result.reshape(1, 1, 8, nh * 2 * D)


def solution(mesh):
    placed = (
        P(("inner", "outer"), None),
        P("inner", None),
        P("inner", None),
        P(("inner", "outer"), "head"),
        P(),
    )
    return jax.shard_map(
        functools.partial(layer, mesh.shape["head"]),
        mesh=mesh,
        in_specs=placed,
        out_specs=P(("inner", "outer"), "head", None, None),
        check_vma=False,
    )
```
